512 devices in a mesh: item: 32 (over y, z_lo, core), grp: 16 (over z_hi, x).
Axes of the slice: x: 4, y: 8, z: 8 (z_hi: 4, z_lo: 2; z = z_hi * 2 + z_lo), core: 2. Of those that a mesh axis runs over, the one named last changes fastest.
Arguments:
- values: bfloat16 [32768, 32], P('item'), may hold values from -40 to 40
- group_map: int32 [32], replicated, may hold values from 0 to 15, as said below
- row_role: int32 [32768], P('item'), may hold values from 0 to 1, as said below
- enc_weight: bfloat16 [32, 192], replicated, may hold values from -4 to 4
- feat_qkv: bfloat16 [192, 576], replicated, may hold values from -0.75 to 0.75
- feat_out: bfloat16 [192, 192], replicated, may hold values from -0.4375 to 0.4375
- feat_gain: float32 [192], replicated, may hold values from 0.5 to 1.5
- item_q: bfloat16 [192, 192], replicated, may hold values from -0.75 to 0.75
- item_kv: bfloat16 [192, 384], replicated, may hold values from -0.75 to 0.75
- item_out: bfloat16 [192, 192], replicated, may hold values from -0.4375 to 0.4375
- item_gain: float32 [192], replicated, may hold values from 0.5 to 1.5
- mlp_in: bfloat16 [192, 768], replicated, may hold values from -0.4375 to 0.4375
- mlp_out: bfloat16 [768, 192], replicated, may hold values from -0.21875 to 0.21875
- mlp_gain: float32 [192], replicated, may hold values from 0.5 to 1.5
Outputs:
- cells_out: bfloat16 [32768, 16, 192], P('item', 'grp')
The draws below stay inside these ranges and needn't reach their ends.
Inputs may be any that keep to these rules, and one draw needn't show every extreme that they name: `row_role`: each aligned block of 1024 rows (the rows of one index of item) holds between 16 and 64 evaluated rows; some block holds exactly 64. `group_map`: each of the 16 groups holds exactly 2 features.
All inputs are finite; a program needn't handle non-finite values.
Results may differ from the reference program's by a relative error of at most 0.0095.
The reference program's roundings to bfloat16 on the way count: a program that leaves them out, or rounds other values in their place, can miss the bound.
Values may be sent and summed in bfloat16 or wider, within the bound.
A program may use at most 64 MiB of HBM per device.

```python
import math
from functools import partial
import jax
import jax.numpy as jnp
from jax import lax

E = 192
HEADS = 6
FF = 768
F = 32
G = 16
GROUP_FEATURES = 2
ROWS_DEV = 1024
EVAL_MAX = 64
ROWS = 32768
N_ITEM = 32


def draw_values(key, part):
    return jnp.clip(jax.random.normal(jax.random.fold_in(key, 1), (ROWS, F), jnp.float32), -4.0, 4.0).astype(jnp.bfloat16)


def draw_group_map(key, part):
    shuffled = jax.random.permutation(jax.random.fold_in(key, 11), F)
    return (shuffled // (F // G)).astype(jnp.int32)


def permute_rows(sub_key):
    return jax.random.permutation(sub_key, ROWS_DEV)


def draw_row_role(key, part):
    device_count = ROWS // ROWS_DEV
    counts = jax.random.randint(jax.random.fold_in(key, 21), (device_count,), ROWS_DEV // 64, ROWS_DEV // 16 + 1)
    busiest = jax.random.randint(jax.random.fold_in(key, 22), (), 0, device_count)
    counts = jnp.where(jnp.arange(device_count) == busiest, ROWS_DEV // 16, counts)
    ranks = jax.vmap(permute_rows)(jax.random.split(jax.random.fold_in(key, 23), device_count))
    return (ranks < counts[:, None]).astype(jnp.int32).reshape(ROWS)


def scatter_about(own_key, dims, spread, limit, kind=jnp.bfloat16):
    values = spread * jax.random.normal(own_key, dims, jnp.float32)
    return jnp.clip(values, min=-limit, max=limit).astype(kind)


def setup_inputs(seed: int = 0) -> dict:
    streams_of = jax.random.split(jax.random.key(seed), 15)
    values = draw_values(jax.random.fold_in(streams_of[14], 71), 0)
    group_map = draw_group_map(jax.random.fold_in(streams_of[14], 71), 0)
    row_role = draw_row_role(jax.random.fold_in(streams_of[14], 71), 0)
    enc_weight = scatter_about(streams_of[3], (F, E), GROUP_FEATURES ** -0.5, 4.0)
    feat_qkv = scatter_about(streams_of[4], (E, 3 * E), (E // 3) ** -0.5, 0.75)
    feat_out = scatter_about(streams_of[5], (E, E), E ** -0.5, 0.4375)
    feat_gain = jnp.clip(1.0 + 0.1 * jax.random.normal(streams_of[6], (E,), jnp.float32), 0.5, 1.5)
    item_q = scatter_about(streams_of[7], (E, E), (E // 3) ** -0.5, 0.75)
    item_kv = scatter_about(streams_of[8], (E, 2 * E), (E // 3) ** -0.5, 0.75)
    item_out = scatter_about(streams_of[9], (E, E), E ** -0.5, 0.4375)
    item_gain = jnp.clip(1.0 + 0.1 * jax.random.normal(streams_of[10], (E,), jnp.float32), 0.5, 1.5)
    mlp_in = scatter_about(streams_of[11], (E, FF), E ** -0.5, 0.4375)
    mlp_out = scatter_about(streams_of[12], (FF, E), FF ** -0.5, 0.21875)
    mlp_gain = jnp.clip(1.0 + 0.1 * jax.random.normal(streams_of[13], (E,), jnp.float32), 0.5, 1.5)
    return {"values": values, "group_map": group_map, "row_role": row_role, "enc_weight": enc_weight, "feat_qkv": feat_qkv, "feat_out": feat_out, "feat_gain": feat_gain, "item_q": item_q, "item_kv": item_kv, "item_out": item_out, "item_gain": item_gain, "mlp_in": mlp_in, "mlp_out": mlp_out, "mlp_gain": mlp_gain}


def layer_norm(inputs, gain):
    average = lax.optimization_barrier(jnp.mean(inputs, axis=-1, keepdims=True))
    centered = inputs - average
    variance = lax.optimization_barrier(jnp.mean(centered * centered, axis=-1, keepdims=True))
    return centered * lax.rsqrt(variance + 1e-05) * gain

def group_attention(row_block, feat_qkv, feat_out, feat_gain):
    row_count, groups, model_width = row_block.shape
    head_dim = model_width // HEADS
    flat = row_block.reshape(row_count * groups, model_width)
    projected = jnp.dot(flat, feat_qkv, preferred_element_type=jnp.float32).astype(jnp.bfloat16)
    projected = projected.astype(jnp.float32).reshape(row_count, groups, 3, HEADS, head_dim)
    queries = projected[:, :, 0]
    key_block = projected[:, :, 1]
    value_block = projected[:, :, 2]
    scores = jnp.einsum('rghd,rkhd->rhgk', queries, key_block, precision=lax.Precision.HIGHEST) / math.sqrt(head_dim)
    top_score = lax.optimization_barrier(jnp.max(scores, axis=-1, keepdims=True))
    weights = jnp.exp(scores - top_score)
    denominator = lax.optimization_barrier(jnp.sum(weights, axis=-1))
    rounded = weights.astype(jnp.bfloat16).astype(jnp.float32)
    mixture = jnp.einsum('rhgk,rkhd->rghd', rounded, value_block, precision=lax.Precision.HIGHEST)
    mixture = mixture / jnp.transpose(denominator, (0, 2, 1))[..., None]
    mixture = mixture.astype(jnp.bfloat16).reshape(row_count * groups, model_width)
    residual = flat.astype(jnp.float32) + jnp.dot(mixture, feat_out, preferred_element_type=jnp.float32)
    return layer_norm(residual, feat_gain).astype(jnp.bfloat16).reshape(row_count, groups, model_width)

def compact_rows(pair):
    row_block, role_block = pair
    is_evaluated = (role_block == 1).astype(jnp.int32)
    position = jnp.cumsum(is_evaluated) - 1
    slot_ids = jnp.arange(EVAL_MAX, dtype=jnp.int32)
    picker = ((position[None, :] == slot_ids[:, None]) & (is_evaluated[None, :] == 1)).astype(jnp.bfloat16)
    chosen = jnp.dot(picker, row_block.reshape(ROWS_DEV, G * E), preferred_element_type=jnp.float32).astype(jnp.bfloat16)
    return (chosen, slot_ids < jnp.sum(is_evaluated))

def attend_group(pair, live):
    queries, key_value = pair
    head_dim = E // HEADS
    scores = jnp.einsum('rhd,khd->rhk', queries, key_value[:, 0], precision=lax.Precision.HIGHEST) / math.sqrt(head_dim)
    masked = jnp.where(live, scores, -1e+30)
    top_score = lax.optimization_barrier(jnp.max(masked, axis=-1, keepdims=True))
    weights = jnp.where(live, jnp.exp(scores - top_score), 0.0)
    denominator = lax.optimization_barrier(jnp.sum(weights, axis=-1))
    rounded = weights.astype(jnp.bfloat16).astype(jnp.float32)
    mixture = jnp.einsum('rhk,khd->rhd', rounded, key_value[:, 1], precision=lax.Precision.HIGHEST)
    return (mixture / denominator[..., None]).astype(jnp.bfloat16)

def item_layer(row_block, group_keys, live, item_q, item_out, item_gain, mlp_in, mlp_out, mlp_gain):
    head_dim = E // HEADS
    flat = row_block.reshape(ROWS_DEV * G, E)
    queries = jnp.dot(flat, item_q, preferred_element_type=jnp.float32).astype(jnp.bfloat16)
    queries = queries.astype(jnp.float32).reshape(ROWS_DEV, G, HEADS, head_dim)
    mixes = lax.map(partial(attend_group, live=live), (jnp.moveaxis(queries, 1, 0), group_keys))
    mixture = jnp.moveaxis(mixes, 0, 1).reshape(ROWS_DEV * G, E)
    residual = flat.astype(jnp.float32) + jnp.dot(mixture, item_out, preferred_element_type=jnp.float32)
    second = layer_norm(residual, item_gain).astype(jnp.bfloat16)
    hidden = jax.nn.gelu(jnp.dot(second, mlp_in, preferred_element_type=jnp.float32), approximate=True).astype(jnp.bfloat16)
    residual = second.astype(jnp.float32) + jnp.dot(hidden, mlp_out, preferred_element_type=jnp.float32)
    return layer_norm(residual, mlp_gain).astype(jnp.bfloat16).reshape(ROWS_DEV, G, E)

def reference(values, group_map, row_role, enc_weight, feat_qkv, feat_out, feat_gain, item_q, item_kv, item_out, item_gain, mlp_in, mlp_out, mlp_gain):
    head_dim = E // HEADS
    selector = (group_map[:, None] == jnp.arange(G, dtype=jnp.int32)[None, :]).astype(jnp.float32)
    embed_table = (selector[:, :, None] * enc_weight.astype(jnp.float32)[:, None, :]).astype(jnp.bfloat16)
    embed_table = embed_table.reshape(F, G * E)
    embedded = jnp.dot(values, embed_table, preferred_element_type=jnp.float32).astype(jnp.bfloat16)
    embedded = embedded.reshape(N_ITEM, ROWS_DEV, G, E)
    first = lax.map(partial(group_attention, feat_qkv=feat_qkv, feat_out=feat_out, feat_gain=feat_gain), embedded)
    chosen, live = lax.map(compact_rows, (first, row_role.reshape(N_ITEM, ROWS_DEV)))
    key_value = jnp.dot(chosen.reshape(N_ITEM * EVAL_MAX * G, E), item_kv, preferred_element_type=jnp.float32).astype(jnp.bfloat16)
    key_value = key_value.astype(jnp.float32).reshape(N_ITEM * EVAL_MAX, G, 2, HEADS, head_dim)
    group_keys = jnp.moveaxis(key_value, 1, 0)
    live = live.reshape(N_ITEM * EVAL_MAX)
    output = lax.map(partial(item_layer, group_keys=group_keys, live=live, item_q=item_q, item_out=item_out, item_gain=item_gain, mlp_in=mlp_in, mlp_out=mlp_out, mlp_gain=mlp_gain), first)
    return output.reshape(ROWS, G, E)
```

```python
import functools
import math

import jax
import jax.numpy as jnp
from jax import lax
from jax.experimental import pallas as pl
from jax.experimental.pallas import tpu as pltpu
from jax.sharding import PartitionSpec as P

HEADS = 6
G = 16
EVAL_MAX = 64
ROW_TILE = 256
COUNT_ROWS = 16
GROUP_TILE = 256
MESH = pl.DeviceIdType.MESH


def layer_norm(inputs, gain):
    average = jnp.mean(inputs, axis=-1, keepdims=True)
    centered = inputs - average
    variance = jnp.mean(centered * centered, axis=-1, keepdims=True)
    return centered * lax.rsqrt(variance + 1e-05) * gain


def embed_table_for(group_map, enc_weight, group_ids):
    selector = (group_map[:, None] == group_ids[None, :]).astype(jnp.float32)
    table = (selector[:, :, None] * enc_weight.astype(jnp.float32)[:, None, :]).astype(jnp.bfloat16)
    return table.reshape(enc_weight.shape[0], group_ids.shape[0] * enc_weight.shape[1])


def split_bf16(x, parts):
    pieces = []
    rest = x
    for _ in range(parts):
        piece = rest.astype(jnp.bfloat16)
        pieces.append(piece)
        rest = rest - piece.astype(jnp.float32)
    return pieces


def group_attention_kernel(v_ref, table_ref, own_ref, wq_ref, wk_ref, wv_ref, wo_ref, gain_ref, o_ref):
    model_width = wq_ref.shape[0]
    head_dim = model_width // HEADS
    scale = 1.0 / math.sqrt(head_dim)
    values = v_ref[...]
    lane_head = lax.broadcasted_iota(jnp.int32, (model_width, 128), 0) // head_dim
    head_lane = lax.broadcasted_iota(jnp.int32, (model_width, 128), 1)
    gather = (lane_head == head_lane).astype(jnp.bfloat16)
    spread_head = lax.broadcasted_iota(jnp.int32, (128, model_width), 0)
    spread_lane = lax.broadcasted_iota(jnp.int32, (128, model_width), 1) // head_dim
    spread = (spread_head == spread_lane).astype(jnp.bfloat16)
    own = jnp.dot(values, own_ref[...], preferred_element_type=jnp.float32).astype(jnp.bfloat16)
    queries = jnp.dot(own, wq_ref[...], preferred_element_type=jnp.float32).astype(jnp.bfloat16)
    queries = queries.astype(jnp.float32)
    scores = []
    vals = []
    for group in range(G):
        embedded = jnp.dot(values, table_ref[group], preferred_element_type=jnp.float32).astype(jnp.bfloat16)
        keys = jnp.dot(embedded, wk_ref[...], preferred_element_type=jnp.float32).astype(jnp.bfloat16)
        vals.append(jnp.dot(embedded, wv_ref[...], preferred_element_type=jnp.float32).astype(jnp.bfloat16))
        products = queries * keys.astype(jnp.float32)
        high, low = split_bf16(products, 2)
        score = jnp.dot(high, gather, preferred_element_type=jnp.float32) + jnp.dot(
            low, gather, preferred_element_type=jnp.float32
        )
        scores.append(score * scale)
    top = scores[0]
    for score in scores[1:]:
        top = jnp.maximum(top, score)
    total = jnp.zeros_like(top)
    mixed = jnp.zeros((values.shape[0], model_width), jnp.float32)
    for group in range(G):
        weight = jnp.exp(scores[group] - top)
        total = total + weight
        spread_weight = jnp.dot(weight.astype(jnp.bfloat16), spread, preferred_element_type=jnp.float32)
        mixed = mixed + spread_weight * vals[group].astype(jnp.float32)
    spread_total = jnp.zeros_like(mixed)
    for piece in split_bf16(total, 3):
        spread_total = spread_total + jnp.dot(piece, spread, preferred_element_type=jnp.float32)
    mixture = (mixed / spread_total).astype(jnp.bfloat16)
    residual = own.astype(jnp.float32) + jnp.dot(mixture, wo_ref[...], preferred_element_type=jnp.float32)
    average = jnp.mean(residual, axis=-1, keepdims=True)
    centered = residual - average
    variance = jnp.mean(centered * centered, axis=-1, keepdims=True)
    normed = centered * lax.rsqrt(variance + 1e-05) * gain_ref[...]
    o_ref[...] = normed.astype(o_ref.dtype)


def group_attention_pallas(values, table, own_table, feat_qkv, feat_out, feat_gain):
    row_count = values.shape[0]
    features, model_width = own_table.shape
    wq = feat_qkv[:, :model_width]
    wk = feat_qkv[:, model_width : 2 * model_width]
    wv = feat_qkv[:, 2 * model_width :]
    full = lambda shape: pl.BlockSpec(shape, lambda i: (0,) * len(shape))
    return pl.pallas_call(
        group_attention_kernel,
        out_shape=jax.ShapeDtypeStruct((row_count, model_width), jnp.bfloat16),
        grid=(row_count // GROUP_TILE,),
        in_specs=[
            pl.BlockSpec((GROUP_TILE, features), lambda i: (i, 0)),
            full((G, features, model_width)),
            full((features, model_width)),
            full((model_width, model_width)),
            full((model_width, model_width)),
            full((model_width, model_width)),
            full((model_width, model_width)),
            full((1, model_width)),
        ],
        out_specs=pl.BlockSpec((GROUP_TILE, model_width), lambda i: (i, 0)),
        cost_estimate=pl.CostEstimate(
            flops=2 * row_count * model_width * (G * (features + 2 * model_width + 3 * 128) + 3 * model_width),
            transcendentals=row_count * G * 128,
            bytes_accessed=2 * row_count * (features + model_width),
        ),
    )(values, table, own_table, wq, wk, wv, feat_out, feat_gain.reshape(1, model_width))


def gather_kernel(chip_count, block_ref, out_ref, send_sems, recv_sems, local_sem, forward_sems):
    me = lax.axis_index("item")
    grp = lax.axis_index("grp")
    core = lax.rem(me, 2)
    chip = me // 2
    partner = me + 1 - 2 * core
    barrier = pltpu.get_barrier_semaphore()
    for step in range(1, chip_count):
        peer = lax.rem(chip + step, chip_count) * 2 + core
        pl.semaphore_signal(barrier, inc=1, device_id=(peer, grp), device_id_type=MESH)
    pl.semaphore_signal(barrier, inc=1, device_id=(partner, grp), device_id_type=MESH)
    pl.semaphore_wait(barrier, chip_count)
    sends = []
    for step in range(1, chip_count):
        peer = lax.rem(chip + step, chip_count) * 2 + core
        copy = pltpu.make_async_remote_copy(
            src_ref=block_ref,
            dst_ref=out_ref.at[core, chip],
            send_sem=send_sems.at[step],
            recv_sem=recv_sems.at[step],
            device_id=(peer, grp),
            device_id_type=MESH,
        )
        copy.start()
        sends.append(copy)
    own = pltpu.make_async_copy(block_ref, out_ref.at[core, chip], local_sem)
    own.start()
    own.wait()
    for copy in sends:
        copy.wait()
    forward = pltpu.make_async_remote_copy(
        src_ref=out_ref.at[core],
        dst_ref=out_ref.at[core],
        send_sem=forward_sems.at[0],
        recv_sem=forward_sems.at[1],
        device_id=(partner, grp),
        device_id_type=MESH,
    )
    forward.start()
    forward.wait()


def gather_items(block, item_count):
    chip_count = item_count // 2
    return pl.pallas_call(
        functools.partial(gather_kernel, chip_count),
        out_shape=jax.ShapeDtypeStruct((2, chip_count) + block.shape, block.dtype),
        in_specs=[pl.BlockSpec(memory_space=pltpu.VMEM)],
        out_specs=pl.BlockSpec(memory_space=pltpu.VMEM),
        scratch_shapes=[
            pltpu.SemaphoreType.DMA((chip_count,)),
            pltpu.SemaphoreType.DMA((chip_count,)),
            pltpu.SemaphoreType.DMA(()),
            pltpu.SemaphoreType.DMA((2,)),
        ],
        compiler_params=pltpu.CompilerParams(collective_id=0, has_side_effects=True),
    )(block)


def row_attention_kernel(q_ref, kt_ref, v_ref, o_ref):
    model_width = q_ref.shape[1]
    heads = HEADS
    head_dim = 32
    scale = 1.0 / math.sqrt(head_dim)
    queries = q_ref[...]
    lane = lax.broadcasted_iota(jnp.int32, (1, model_width), 1)
    extra = lane == heads * head_dim
    lane_head = lane // head_dim
    out = jnp.zeros(o_ref.shape, jnp.float32)
    for head in range(heads):
        own = lane_head == head
        head_queries = jnp.where(own | extra, queries, jnp.zeros_like(queries))
        scores = jnp.dot(head_queries, kt_ref[...], preferred_element_type=jnp.float32) * scale
        top = jnp.max(scores, axis=-1, keepdims=True)
        weights = jnp.exp(scores - top)
        mixed = jnp.dot(weights.astype(jnp.bfloat16), v_ref[...], preferred_element_type=jnp.float32)
        total = mixed[:, heads * head_dim : heads * head_dim + 1]
        out = jnp.where(own, mixed / total, out)
    o_ref[...] = out.astype(o_ref.dtype)


def row_attention(queries, keys_t, vals):
    row_count, lanes = queries.shape
    key_count = vals.shape[0]
    return pl.pallas_call(
        row_attention_kernel,
        out_shape=jax.ShapeDtypeStruct((row_count, lanes), jnp.bfloat16),
        grid=(row_count // ROW_TILE,),
        in_specs=[
            pl.BlockSpec((ROW_TILE, lanes), lambda i: (i, 0)),
            pl.BlockSpec((lanes, key_count), lambda i: (0, 0)),
            pl.BlockSpec((key_count, lanes), lambda i: (0, 0)),
        ],
        out_specs=pl.BlockSpec((ROW_TILE, lanes), lambda i: (i, 0)),
        cost_estimate=pl.CostEstimate(
            flops=4 * HEADS * row_count * key_count * lanes,
            transcendentals=HEADS * row_count * key_count,
            bytes_accessed=2 * (2 * row_count * lanes + 2 * key_count * lanes),
        ),
    )(queries, keys_t, vals)


def per_device(
    values,
    group_map,
    row_role,
    enc_weight,
    feat_qkv,
    feat_out,
    feat_gain,
    item_q,
    item_kv,
    item_out,
    item_gain,
    mlp_in,
    mlp_out,
    mlp_gain,
):
    row_count = values.shape[0]
    model_width = enc_weight.shape[1]
    head_dim = model_width // HEADS
    grp_count = lax.axis_size("grp")
    local_groups = G // grp_count
    own_groups = lax.axis_index("grp") * local_groups + jnp.arange(local_groups, dtype=jnp.int32)
    table = embed_table_for(group_map, enc_weight, jnp.arange(G, dtype=jnp.int32))
    table = jnp.transpose(table.reshape(enc_weight.shape[0], G, model_width), (1, 0, 2))
    own_table = embed_table_for(group_map, enc_weight, own_groups)
    flat_first = group_attention_pallas(values, table, own_table, feat_qkv, feat_out, feat_gain)
    first = flat_first.reshape(row_count, local_groups, model_width)
    padded = 256
    item_q_wide = jnp.zeros((model_width, padded), item_q.dtype).at[:, :model_width].set(item_q)
    unit_lane = (jnp.arange(padded, dtype=jnp.int32) == model_width).astype(jnp.float32)
    queries = jnp.dot(flat_first, item_q_wide, preferred_element_type=jnp.float32)
    queries = (queries + unit_lane[None, :]).astype(jnp.bfloat16)
    is_evaluated = (row_role == 1).astype(jnp.int32)
    position = jnp.cumsum(is_evaluated) - 1
    slot_ids = jnp.arange(EVAL_MAX, dtype=jnp.int32)
    picker = ((position[None, :] == slot_ids[:, None]) & (is_evaluated[None, :] == 1)).astype(
        jnp.bfloat16
    )
    chosen = jnp.dot(
        picker, first.reshape(row_count, local_groups * model_width), preferred_element_type=jnp.float32
    ).astype(jnp.bfloat16)
    chosen = chosen.reshape(EVAL_MAX * local_groups, model_width)
    count = jnp.sum(is_evaluated).astype(jnp.bfloat16)
    lanes = 128
    dense = chosen.reshape(EVAL_MAX * model_width // lanes, lanes)
    count_rows = jnp.zeros((COUNT_ROWS, lanes), jnp.bfloat16).at[0, 0].set(count)
    payload = gather_items(jnp.concatenate([dense, count_rows], axis=0), lax.axis_size("item"))
    shard_count = payload.shape[0] * payload.shape[1]
    payload = payload.reshape(shard_count, dense.shape[0] + COUNT_ROWS, lanes)
    counts = payload[:, dense.shape[0], 0].astype(jnp.int32)
    bias = jnp.where(slot_ids[None, :] < counts[:, None], 0.0, -1e30).reshape(1, -1)
    gathered = payload[:, : dense.shape[0]].reshape(shard_count * EVAL_MAX, model_width)
    keys_t = jnp.einsum(
        "cn,sc->ns", item_kv[:, :model_width], gathered, preferred_element_type=jnp.float32
    ).astype(jnp.bfloat16)
    keys_t = jnp.concatenate(
        [keys_t, bias.astype(jnp.bfloat16), jnp.zeros((padded - model_width - 1, keys_t.shape[1]), jnp.bfloat16)],
        axis=0,
    )
    vals = jnp.dot(
        gathered, item_kv[:, model_width:], preferred_element_type=jnp.float32
    ).astype(jnp.bfloat16)
    vals = jnp.concatenate(
        [vals, jnp.ones((vals.shape[0], 1), jnp.bfloat16), jnp.zeros((vals.shape[0], padded - model_width - 1), jnp.bfloat16)],
        axis=1,
    )
    mixture = row_attention(queries, keys_t, vals)[:, :model_width]
    residual = flat_first.astype(jnp.float32) + jnp.dot(
        mixture, item_out, preferred_element_type=jnp.float32
    )
    second = layer_norm(residual, item_gain).astype(jnp.bfloat16)
    hidden = jax.nn.gelu(
        jnp.dot(second, mlp_in, preferred_element_type=jnp.float32), approximate=True
    ).astype(jnp.bfloat16)
    residual = second.astype(jnp.float32) + jnp.dot(
        hidden, mlp_out, preferred_element_type=jnp.float32
    )
    return (
        layer_norm(residual, mlp_gain)
        .astype(jnp.bfloat16)
        .reshape(row_count, local_groups, model_width)
    )


def solution(mesh):
    in_specs = (
        P("item", None),
        P(),
        P("item"),
        P(),
        P(),
        P(),
        P(),
        P(),
        P(),
        P(),
        P(),
        P(),
        P(),
        P(),
    )
    out_specs = P("item", "grp", None)
    return jax.shard_map(
        per_device, mesh=mesh, in_specs=in_specs, out_specs=out_specs, check_vma=False
    )
```

```python
import functools
import math

import jax
import jax.numpy as jnp
from jax import lax
from jax.experimental import pallas as pl
from jax.experimental.pallas import tpu as pltpu
from jax.sharding import PartitionSpec as P

HEADS = 6
G = 16
EVAL_MAX = 64
ROW_TILE = 256
COUNT_ROWS = 16
GROUP_TILE = 256
MESH = pl.DeviceIdType.MESH


def layer_norm(inputs, gain):
    average = jnp.mean(inputs, axis=-1, keepdims=True)
    centered = inputs - average
    variance = jnp.mean(centered * centered, axis=-1, keepdims=True)
    return centered * lax.rsqrt(variance + 1e-05) * gain


def embed_table_for(group_map, enc_weight, group_ids):
    selector = (group_map[:, None] == group_ids[None, :]).astype(jnp.float32)
    table = (selector[:, :, None] * enc_weight.astype(jnp.float32)[:, None, :]).astype(jnp.bfloat16)
    return table.reshape(enc_weight.shape[0], group_ids.shape[0] * enc_weight.shape[1])


def split_bf16(x, parts):
    pieces = []
    rest = x
    for _ in range(parts):
        piece = rest.astype(jnp.bfloat16)
        pieces.append(piece)
        rest = rest - piece.astype(jnp.float32)
    return pieces


def group_attention_kernel(v_ref, table_ref, own_ref, wq_ref, wk_ref, wv_ref, wo_ref, gain_ref, o_ref):
    o_ref[...] = group_attention_rows(
        v_ref[...], table_ref, own_ref, wq_ref, wk_ref, wv_ref, wo_ref, gain_ref
    ).astype(o_ref.dtype)


def group_attention_rows(values, table_ref, own_ref, wq_ref, wk_ref, wv_ref, wo_ref, gain_ref):
    model_width = wq_ref.shape[0]
    head_dim = model_width // HEADS
    scale = 1.0 / math.sqrt(head_dim)
    lane_head = lax.broadcasted_iota(jnp.int32, (model_width, 128), 0) // head_dim
    head_lane = lax.broadcasted_iota(jnp.int32, (model_width, 128), 1)
    gather = (lane_head == head_lane).astype(jnp.bfloat16)
    spread_head = lax.broadcasted_iota(jnp.int32, (128, model_width), 0)
    spread_lane = lax.broadcasted_iota(jnp.int32, (128, model_width), 1) // head_dim
    spread = (spread_head == spread_lane).astype(jnp.bfloat16)
    own = jnp.dot(values, own_ref[...], preferred_element_type=jnp.float32).astype(jnp.bfloat16)
    queries = jnp.dot(own, wq_ref[...], preferred_element_type=jnp.float32).astype(jnp.bfloat16)
    queries = queries.astype(jnp.float32)
    scores = []
    vals = []
    for group in range(G):
        embedded = jnp.dot(values, table_ref[group], preferred_element_type=jnp.float32).astype(jnp.bfloat16)
        keys = jnp.dot(embedded, wk_ref[...], preferred_element_type=jnp.float32).astype(jnp.bfloat16)
        vals.append(jnp.dot(embedded, wv_ref[...], preferred_element_type=jnp.float32).astype(jnp.bfloat16))
        products = queries * keys.astype(jnp.float32)
        high, low = split_bf16(products, 2)
        score = jnp.dot(high, gather, preferred_element_type=jnp.float32) + jnp.dot(
            low, gather, preferred_element_type=jnp.float32
        )
        scores.append(score * scale)
    top = scores[0]
    for score in scores[1:]:
        top = jnp.maximum(top, score)
    total = jnp.zeros_like(top)
    mixed = jnp.zeros((values.shape[0], model_width), jnp.float32)
    for group in range(G):
        weight = jnp.exp(scores[group] - top)
        total = total + weight
        spread_weight = jnp.dot(weight.astype(jnp.bfloat16), spread, preferred_element_type=jnp.float32)
        mixed = mixed + spread_weight * vals[group].astype(jnp.float32)
    spread_total = jnp.zeros_like(mixed)
    for piece in split_bf16(total, 3):
        spread_total = spread_total + jnp.dot(piece, spread, preferred_element_type=jnp.float32)
    mixture = (mixed / spread_total).astype(jnp.bfloat16)
    residual = own.astype(jnp.float32) + jnp.dot(mixture, wo_ref[...], preferred_element_type=jnp.float32)
    average = jnp.mean(residual, axis=-1, keepdims=True)
    centered = residual - average
    variance = jnp.mean(centered * centered, axis=-1, keepdims=True)
    return centered * lax.rsqrt(variance + 1e-05) * gain_ref[...]


def group_attention_pallas(values, table, own_table, feat_qkv, feat_out, feat_gain, tile):
    row_count = values.shape[0]
    features, model_width = own_table.shape
    wq = feat_qkv[:, :model_width]
    wk = feat_qkv[:, model_width : 2 * model_width]
    wv = feat_qkv[:, 2 * model_width :]
    full = lambda shape: pl.BlockSpec(shape, lambda i: (0,) * len(shape))
    return pl.pallas_call(
        group_attention_kernel,
        out_shape=jax.ShapeDtypeStruct((row_count, model_width), jnp.bfloat16),
        grid=(row_count // tile,),
        in_specs=[
            pl.BlockSpec((tile, features), lambda i: (i, 0)),
            full((G, features, model_width)),
            full((features, model_width)),
            full((model_width, model_width)),
            full((model_width, model_width)),
            full((model_width, model_width)),
            full((model_width, model_width)),
            full((1, model_width)),
        ],
        out_specs=pl.BlockSpec((tile, model_width), lambda i: (i, 0)),
        cost_estimate=pl.CostEstimate(
            flops=2 * row_count * model_width * (G * (features + 2 * model_width + 3 * 128) + 3 * model_width),
            transcendentals=row_count * G * 128,
            bytes_accessed=2 * row_count * (features + model_width),
        ),
    )(values, table, own_table, wq, wk, wv, feat_out, feat_gain.reshape(1, model_width))


def gather_kernel(
    chip_count, block_ref, v_ref, table_ref, own_ref, wq_ref, wk_ref, wv_ref, wo_ref, gain_ref,
    out_ref, first_ref, send_sems, recv_sems, local_sem, forward_sems,
):
    me = lax.axis_index("item")
    grp = lax.axis_index("grp")
    core = lax.rem(me, 2)
    chip = me // 2
    partner = me + 1 - 2 * core
    barrier = pltpu.get_barrier_semaphore()
    for step in range(1, chip_count):
        peer = lax.rem(chip + step, chip_count) * 2 + core
        pl.semaphore_signal(barrier, inc=1, device_id=(peer, grp), device_id_type=MESH)
    pl.semaphore_signal(barrier, inc=1, device_id=(partner, grp), device_id_type=MESH)
    pl.semaphore_wait(barrier, chip_count)
    sends = []
    for step in range(1, chip_count):
        peer = lax.rem(chip + step, chip_count) * 2 + core
        copy = pltpu.make_async_remote_copy(
            src_ref=block_ref,
            dst_ref=out_ref.at[core, chip],
            send_sem=send_sems.at[step],
            recv_sem=recv_sems.at[step],
            device_id=(peer, grp),
            device_id_type=MESH,
        )
        copy.start()
        sends.append(copy)
    own = pltpu.make_async_copy(block_ref, out_ref.at[core, chip], local_sem)
    own.start()

    def tile(index, carry):
        rows = pl.ds(pl.multiple_of(index * GROUP_TILE, GROUP_TILE), GROUP_TILE)
        first_ref[rows, :] = group_attention_rows(
            v_ref[rows, :], table_ref, own_ref, wq_ref, wk_ref, wv_ref, wo_ref, gain_ref
        ).astype(first_ref.dtype)
        return carry

    lax.fori_loop(0, first_ref.shape[0] // GROUP_TILE, tile, 0)
    own.wait()
    for copy in sends:
        copy.wait()
    forward = pltpu.make_async_remote_copy(
        src_ref=out_ref.at[core],
        dst_ref=out_ref.at[core],
        send_sem=forward_sems.at[0],
        recv_sem=forward_sems.at[1],
        device_id=(partner, grp),
        device_id_type=MESH,
    )
    forward.start()
    forward.wait()


def gather_items(block, item_count, values, table, own_table, feat_qkv, feat_out, feat_gain):
    chip_count = item_count // 2
    model_width = own_table.shape[1]
    vmem = pl.BlockSpec(memory_space=pltpu.VMEM)
    return pl.pallas_call(
        functools.partial(gather_kernel, chip_count),
        out_shape=(
            jax.ShapeDtypeStruct((2, chip_count) + block.shape, block.dtype),
            jax.ShapeDtypeStruct((values.shape[0], model_width), jnp.bfloat16),
        ),
        in_specs=[vmem] * 9,
        out_specs=(vmem, vmem),
        scratch_shapes=[
            pltpu.SemaphoreType.DMA((chip_count,)),
            pltpu.SemaphoreType.DMA((chip_count,)),
            pltpu.SemaphoreType.DMA(()),
            pltpu.SemaphoreType.DMA((2,)),
        ],
        compiler_params=pltpu.CompilerParams(collective_id=0, has_side_effects=True),
    )(
        block,
        values,
        table,
        own_table,
        feat_qkv[:, :model_width],
        feat_qkv[:, model_width : 2 * model_width],
        feat_qkv[:, 2 * model_width :],
        feat_out,
        feat_gain.reshape(1, model_width),
    )


def row_attention_kernel(q_ref, kt_ref, v_ref, o_ref):
    model_width = q_ref.shape[1]
    heads = HEADS
    head_dim = 32
    scale = 1.0 / math.sqrt(head_dim)
    queries = q_ref[...]
    lane = lax.broadcasted_iota(jnp.int32, (1, model_width), 1)
    extra = lane == heads * head_dim
    lane_head = lane // head_dim
    out = jnp.zeros(o_ref.shape, jnp.float32)
    for head in range(heads):
        own = lane_head == head
        head_queries = jnp.where(own | extra, queries, jnp.zeros_like(queries))
        scores = jnp.dot(head_queries, kt_ref[...], preferred_element_type=jnp.float32) * scale
        top = jnp.max(scores, axis=-1, keepdims=True)
        weights = jnp.exp(scores - top)
        mixed = jnp.dot(weights.astype(jnp.bfloat16), v_ref[...], preferred_element_type=jnp.float32)
        total = mixed[:, heads * head_dim : heads * head_dim + 1]
        out = jnp.where(own, mixed / total, out)
    o_ref[...] = out.astype(o_ref.dtype)


def row_attention(queries, keys_t, vals):
    row_count, lanes = queries.shape
    key_count = vals.shape[0]
    return pl.pallas_call(
        row_attention_kernel,
        out_shape=jax.ShapeDtypeStruct((row_count, lanes), jnp.bfloat16),
        grid=(row_count // ROW_TILE,),
        in_specs=[
            pl.BlockSpec((ROW_TILE, lanes), lambda i: (i, 0)),
            pl.BlockSpec((lanes, key_count), lambda i: (0, 0)),
            pl.BlockSpec((key_count, lanes), lambda i: (0, 0)),
        ],
        out_specs=pl.BlockSpec((ROW_TILE, lanes), lambda i: (i, 0)),
        cost_estimate=pl.CostEstimate(
            flops=4 * HEADS * row_count * key_count * lanes,
            transcendentals=HEADS * row_count * key_count,
            bytes_accessed=2 * (2 * row_count * lanes + 2 * key_count * lanes),
        ),
    )(queries, keys_t, vals)


def per_device(
    values,
    group_map,
    row_role,
    enc_weight,
    feat_qkv,
    feat_out,
    feat_gain,
    item_q,
    item_kv,
    item_out,
    item_gain,
    mlp_in,
    mlp_out,
    mlp_gain,
):
    row_count = values.shape[0]
    model_width = enc_weight.shape[1]
    head_dim = model_width // HEADS
    grp_count = lax.axis_size("grp")
    local_groups = G // grp_count
    own_groups = lax.axis_index("grp") * local_groups + jnp.arange(local_groups, dtype=jnp.int32)
    table = embed_table_for(group_map, enc_weight, jnp.arange(G, dtype=jnp.int32))
    table = jnp.transpose(table.reshape(enc_weight.shape[0], G, model_width), (1, 0, 2))
    own_table = embed_table_for(group_map, enc_weight, own_groups)
    is_evaluated = (row_role == 1).astype(jnp.int32)
    position = jnp.cumsum(is_evaluated) - 1
    slot_ids = jnp.arange(EVAL_MAX, dtype=jnp.int32)
    picker = ((position[None, :] == slot_ids[:, None]) & (is_evaluated[None, :] == 1)).astype(
        jnp.bfloat16
    )
    chosen_values = jnp.dot(picker, values, preferred_element_type=jnp.float32).astype(values.dtype)
    chosen = group_attention_pallas(
        chosen_values, table, own_table, feat_qkv, feat_out, feat_gain, EVAL_MAX
    )
    chosen = jnp.where((slot_ids < jnp.sum(is_evaluated))[:, None], chosen, jnp.zeros_like(chosen))
    count = jnp.sum(is_evaluated).astype(jnp.bfloat16)
    lanes = 128
    dense = chosen.reshape(EVAL_MAX * model_width // lanes, lanes)
    count_rows = jnp.zeros((COUNT_ROWS, lanes), jnp.bfloat16).at[0, 0].set(count)
    payload, flat_first = gather_items(
        jnp.concatenate([dense, count_rows], axis=0),
        lax.axis_size("item"),
        values,
        table,
        own_table,
        feat_qkv,
        feat_out,
        feat_gain,
    )
    padded = 256
    item_q_wide = jnp.zeros((model_width, padded), item_q.dtype).at[:, :model_width].set(item_q)
    unit_lane = (jnp.arange(padded, dtype=jnp.int32) == model_width).astype(jnp.float32)
    queries = jnp.dot(flat_first, item_q_wide, preferred_element_type=jnp.float32)
    queries = (queries + unit_lane[None, :]).astype(jnp.bfloat16)
    shard_count = payload.shape[0] * payload.shape[1]
    payload = payload.reshape(shard_count, dense.shape[0] + COUNT_ROWS, lanes)
    counts = payload[:, dense.shape[0], 0].astype(jnp.int32)
    bias = jnp.where(slot_ids[None, :] < counts[:, None], 0.0, -1e30).reshape(1, -1)
    gathered = payload[:, : dense.shape[0]].reshape(shard_count * EVAL_MAX, model_width)
    keys_t = jnp.einsum(
        "cn,sc->ns", item_kv[:, :model_width], gathered, preferred_element_type=jnp.float32
    ).astype(jnp.bfloat16)
    keys_t = jnp.concatenate(
        [keys_t, bias.astype(jnp.bfloat16), jnp.zeros((padded - model_width - 1, keys_t.shape[1]), jnp.bfloat16)],
        axis=0,
    )
    vals = jnp.dot(
        gathered, item_kv[:, model_width:], preferred_element_type=jnp.float32
    ).astype(jnp.bfloat16)
    vals = jnp.concatenate(
        [vals, jnp.ones((vals.shape[0], 1), jnp.bfloat16), jnp.zeros((vals.shape[0], padded - model_width - 1), jnp.bfloat16)],
        axis=1,
    )
    mixture = row_attention(queries, keys_t, vals)[:, :model_width]
    residual = flat_first.astype(jnp.float32) + jnp.dot(
        mixture, item_out, preferred_element_type=jnp.float32
    )
    second = layer_norm(residual, item_gain).astype(jnp.bfloat16)
    hidden = jax.nn.gelu(
        jnp.dot(second, mlp_in, preferred_element_type=jnp.float32), approximate=True
    ).astype(jnp.bfloat16)
    residual = second.astype(jnp.float32) + jnp.dot(
        hidden, mlp_out, preferred_element_type=jnp.float32
    )
    return (
        layer_norm(residual, mlp_gain)
        .astype(jnp.bfloat16)
        .reshape(row_count, local_groups, model_width)
    )


def solution(mesh):
    in_specs = (
        P("item", None),
        P(),
        P("item"),
        P(),
        P(),
        P(),
        P(),
        P(),
        P(),
        P(),
        P(),
        P(),
        P(),
        P(),
    )
    out_specs = P("item", "grp", None)
    return jax.shard_map(
        per_device, mesh=mesh, in_specs=in_specs, out_specs=out_specs, check_vma=False
    )
```

```python
import functools
import math

import jax
import jax.numpy as jnp
from jax import lax
from jax.experimental import pallas as pl
from jax.experimental.pallas import tpu as pltpu
from jax.sharding import PartitionSpec as P

HEADS = 6
G = 16
EVAL_MAX = 64
ROW_TILE = 256
COUNT_ROWS = 16
GROUP_TILE = 128
MESH = pl.DeviceIdType.MESH


def layer_norm(inputs, gain):
    average = jnp.mean(inputs, axis=-1, keepdims=True)
    centered = inputs - average
    variance = jnp.mean(centered * centered, axis=-1, keepdims=True)
    return centered * lax.rsqrt(variance + 1e-05) * gain


def embed_table_for(group_map, enc_weight, group_ids):
    selector = (group_map[:, None] == group_ids[None, :]).astype(jnp.float32)
    table = (selector[:, :, None] * enc_weight.astype(jnp.float32)[:, None, :]).astype(jnp.bfloat16)
    return table.reshape(enc_weight.shape[0], group_ids.shape[0] * enc_weight.shape[1])


def split_bf16(x, parts):
    pieces = []
    rest = x
    for _ in range(parts):
        piece = rest.astype(jnp.bfloat16)
        pieces.append(piece)
        rest = rest - piece.astype(jnp.float32)
    return pieces


def group_attention_kernel(v_ref, table_ref, own_ref, wq_ref, wk_ref, wv_ref, wo_ref, gain_ref, o_ref):
    o_ref[...] = group_attention_rows(
        v_ref[...], table_ref, own_ref, wq_ref, wk_ref, wv_ref, wo_ref, gain_ref
    ).astype(o_ref.dtype)


def group_attention_rows(values, table_ref, own_ref, wq_ref, wk_ref, wv_ref, wo_ref, gain_ref):
    rows = values.shape[0]
    model_width = wq_ref.shape[0]
    wide = wk_ref.shape[0]
    head_dim = model_width // HEADS
    scale = 1.0 / math.sqrt(head_dim)
    lane_head = lax.broadcasted_iota(jnp.int32, (model_width, 128), 0) // head_dim
    head_lane = lax.broadcasted_iota(jnp.int32, (model_width, 128), 1)
    gather = (lane_head == head_lane).astype(jnp.bfloat16)
    spread_head = lax.broadcasted_iota(jnp.int32, (128, model_width), 0)
    spread_lane = lax.broadcasted_iota(jnp.int32, (128, model_width), 1) // head_dim
    spread = (spread_head == spread_lane).astype(jnp.bfloat16)
    own = jnp.dot(values, own_ref[...], preferred_element_type=jnp.float32).astype(jnp.bfloat16)
    queries = jnp.dot(own, wq_ref[...], preferred_element_type=jnp.float32).astype(jnp.bfloat16)
    queries = queries.astype(jnp.float32)
    embedded = jnp.dot(values, table_ref[...], preferred_element_type=jnp.float32).astype(jnp.bfloat16)
    stacked = jnp.concatenate([embedded[:, g * wide : (g + 1) * wide] for g in range(G)], axis=0)
    keys = jnp.dot(stacked, wk_ref[...], preferred_element_type=jnp.float32).astype(jnp.bfloat16)
    vals = jnp.dot(stacked, wv_ref[...], preferred_element_type=jnp.float32).astype(jnp.bfloat16)
    products = (keys.astype(jnp.float32).reshape(G, rows, model_width) * queries[None]).reshape(
        G * rows, model_width
    )
    high, low = split_bf16(products, 2)
    scores = jnp.dot(high, gather, preferred_element_type=jnp.float32) + jnp.dot(
        low, gather, preferred_element_type=jnp.float32
    )
    scores = scores.reshape(G, rows, 128) * scale
    top = jnp.max(scores, axis=0)
    weights = jnp.exp(scores - top[None])
    total = jnp.sum(weights, axis=0)
    spread_weight = jnp.dot(
        weights.reshape(G * rows, 128).astype(jnp.bfloat16), spread, preferred_element_type=jnp.float32
    )
    mixed = jnp.sum(
        (spread_weight * vals.astype(jnp.float32)).reshape(G, rows, model_width), axis=0
    )
    spread_total = jnp.zeros_like(mixed)
    for piece in split_bf16(total, 3):
        spread_total = spread_total + jnp.dot(piece, spread, preferred_element_type=jnp.float32)
    mixture = (mixed / spread_total).astype(jnp.bfloat16)
    residual = own.astype(jnp.float32) + jnp.dot(mixture, wo_ref[...], preferred_element_type=jnp.float32)
    average = jnp.mean(residual, axis=-1, keepdims=True)
    centered = residual - average
    variance = jnp.mean(centered * centered, axis=-1, keepdims=True)
    return centered * lax.rsqrt(variance + 1e-05) * gain_ref[...]


def pad_rows(matrix, rows):
    return jnp.concatenate(
        [matrix, jnp.zeros((rows - matrix.shape[0], matrix.shape[1]), matrix.dtype)], axis=0
    )


def group_attention_pallas(values, table, own_table, weights, tile):
    row_count, features = values.shape
    model_width = own_table.shape[1]
    full = lambda array: pl.BlockSpec(array.shape, lambda i: (0,) * array.ndim)
    return pl.pallas_call(
        group_attention_kernel,
        out_shape=jax.ShapeDtypeStruct((row_count, model_width), jnp.bfloat16),
        grid=(row_count // tile,),
        in_specs=[pl.BlockSpec((tile, features), lambda i: (i, 0))]
        + [full(array) for array in (table, own_table) + weights],
        out_specs=pl.BlockSpec((tile, model_width), lambda i: (i, 0)),
        cost_estimate=pl.CostEstimate(
            flops=2 * row_count * model_width * (G * (features + 2 * model_width + 3 * 128) + 3 * model_width),
            transcendentals=row_count * G * 128,
            bytes_accessed=2 * row_count * (features + model_width),
        ),
    )(values, table, own_table, *weights)


def gather_kernel(
    chip_count, block_ref, v_ref, table_ref, own_ref, wq_ref, wk_ref, wv_ref, wo_ref, gain_ref,
    out_ref, first_ref, send_sems, recv_sems, local_sem, forward_sems,
):
    me = lax.axis_index("item")
    grp = lax.axis_index("grp")
    core = lax.rem(me, 2)
    chip = me // 2
    partner = me + 1 - 2 * core
    barrier = pltpu.get_barrier_semaphore()
    for step in range(1, chip_count):
        peer = lax.rem(chip + step, chip_count) * 2 + core
        pl.semaphore_signal(barrier, inc=1, device_id=(peer, grp), device_id_type=MESH)
    pl.semaphore_signal(barrier, inc=1, device_id=(partner, grp), device_id_type=MESH)
    pl.semaphore_wait(barrier, chip_count)
    sends = []
    for step in range(1, chip_count):
        peer = lax.rem(chip + step, chip_count) * 2 + core
        copy = pltpu.make_async_remote_copy(
            src_ref=block_ref,
            dst_ref=out_ref.at[core, chip],
            send_sem=send_sems.at[step],
            recv_sem=recv_sems.at[step],
            device_id=(peer, grp),
            device_id_type=MESH,
        )
        copy.start()
        sends.append(copy)
    own = pltpu.make_async_copy(block_ref, out_ref.at[core, chip], local_sem)
    own.start()

    def tile(index, carry):
        rows = pl.ds(pl.multiple_of(index * GROUP_TILE, GROUP_TILE), GROUP_TILE)
        first_ref[rows, :] = group_attention_rows(
            v_ref[rows, :], table_ref, own_ref, wq_ref, wk_ref, wv_ref, wo_ref, gain_ref
        ).astype(first_ref.dtype)
        return carry

    lax.fori_loop(0, first_ref.shape[0] // GROUP_TILE, tile, 0)
    own.wait()
    for copy in sends:
        copy.wait()
    forward = pltpu.make_async_remote_copy(
        src_ref=out_ref.at[core],
        dst_ref=out_ref.at[core],
        send_sem=forward_sems.at[0],
        recv_sem=forward_sems.at[1],
        device_id=(partner, grp),
        device_id_type=MESH,
    )
    forward.start()
    forward.wait()


def gather_items(block, item_count, values, table, own_table, weights):
    chip_count = item_count // 2
    model_width = own_table.shape[1]
    vmem = pl.BlockSpec(memory_space=pltpu.VMEM)
    return pl.pallas_call(
        functools.partial(gather_kernel, chip_count),
        out_shape=(
            jax.ShapeDtypeStruct((2, chip_count) + block.shape, block.dtype),
            jax.ShapeDtypeStruct((values.shape[0], model_width), jnp.bfloat16),
        ),
        in_specs=[vmem] * 9,
        out_specs=(vmem, vmem),
        scratch_shapes=[
            pltpu.SemaphoreType.DMA((chip_count,)),
            pltpu.SemaphoreType.DMA((chip_count,)),
            pltpu.SemaphoreType.DMA(()),
            pltpu.SemaphoreType.DMA((2,)),
        ],
        compiler_params=pltpu.CompilerParams(collective_id=0, has_side_effects=True),
    )(block, values, table, own_table, *weights)


def row_attention_kernel(q_ref, kt_ref, v_ref, o_ref):
    model_width = q_ref.shape[1]
    heads = HEADS
    head_dim = 32
    scale = 1.0 / math.sqrt(head_dim)
    queries = q_ref[...]
    lane = lax.broadcasted_iota(jnp.int32, (1, model_width), 1)
    extra = lane == heads * head_dim
    lane_head = lane // head_dim
    out = jnp.zeros(o_ref.shape, jnp.float32)
    for head in range(heads):
        own = lane_head == head
        head_queries = jnp.where(own | extra, queries, jnp.zeros_like(queries))
        scores = jnp.dot(head_queries, kt_ref[...], preferred_element_type=jnp.float32) * scale
        top = jnp.max(scores, axis=-1, keepdims=True)
        weights = jnp.exp(scores - top)
        mixed = jnp.dot(weights.astype(jnp.bfloat16), v_ref[...], preferred_element_type=jnp.float32)
        total = mixed[:, heads * head_dim : heads * head_dim + 1]
        out = jnp.where(own, mixed / total, out)
    o_ref[...] = out.astype(o_ref.dtype)


def row_attention(queries, keys_t, vals):
    row_count, lanes = queries.shape
    key_count = vals.shape[0]
    return pl.pallas_call(
        row_attention_kernel,
        out_shape=jax.ShapeDtypeStruct((row_count, lanes), jnp.bfloat16),
        grid=(row_count // ROW_TILE,),
        in_specs=[
            pl.BlockSpec((ROW_TILE, lanes), lambda i: (i, 0)),
            pl.BlockSpec((lanes, key_count), lambda i: (0, 0)),
            pl.BlockSpec((key_count, lanes), lambda i: (0, 0)),
        ],
        out_specs=pl.BlockSpec((ROW_TILE, lanes), lambda i: (i, 0)),
        cost_estimate=pl.CostEstimate(
            flops=4 * HEADS * row_count * key_count * lanes,
            transcendentals=HEADS * row_count * key_count,
            bytes_accessed=2 * (2 * row_count * lanes + 2 * key_count * lanes),
        ),
    )(queries, keys_t, vals)


def per_device(
    values,
    group_map,
    row_role,
    enc_weight,
    feat_qkv,
    feat_out,
    feat_gain,
    item_q,
    item_kv,
    item_out,
    item_gain,
    mlp_in,
    mlp_out,
    mlp_gain,
):
    row_count = values.shape[0]
    model_width = enc_weight.shape[1]
    head_dim = model_width // HEADS
    grp_count = lax.axis_size("grp")
    local_groups = G // grp_count
    own_groups = lax.axis_index("grp") * local_groups + jnp.arange(local_groups, dtype=jnp.int32)
    wide = 256
    table = embed_table_for(group_map, enc_weight, jnp.arange(G, dtype=jnp.int32))
    table = table.reshape(enc_weight.shape[0], G, model_width)
    table = jnp.concatenate(
        [table, jnp.zeros((enc_weight.shape[0], G, wide - model_width), table.dtype)], axis=2
    ).reshape(enc_weight.shape[0], G * wide)
    own_table = embed_table_for(group_map, enc_weight, own_groups)
    weights = (
        feat_qkv[:, :model_width],
        pad_rows(feat_qkv[:, model_width : 2 * model_width], wide),
        pad_rows(feat_qkv[:, 2 * model_width :], wide),
        feat_out,
        feat_gain.reshape(1, model_width),
    )
    is_evaluated = (row_role == 1).astype(jnp.int32)
    position = jnp.cumsum(is_evaluated) - 1
    slot_ids = jnp.arange(EVAL_MAX, dtype=jnp.int32)
    picker = ((position[None, :] == slot_ids[:, None]) & (is_evaluated[None, :] == 1)).astype(
        jnp.bfloat16
    )
    chosen_values = jnp.dot(picker, values, preferred_element_type=jnp.float32).astype(values.dtype)
    chosen = group_attention_pallas(chosen_values, table, own_table, weights, EVAL_MAX)
    chosen = jnp.where((slot_ids < jnp.sum(is_evaluated))[:, None], chosen, jnp.zeros_like(chosen))
    count = jnp.sum(is_evaluated).astype(jnp.bfloat16)
    lanes = 128
    dense = chosen.reshape(EVAL_MAX * model_width // lanes, lanes)
    count_rows = jnp.zeros((COUNT_ROWS, lanes), jnp.bfloat16).at[0, 0].set(count)
    payload, flat_first = gather_items(
        jnp.concatenate([dense, count_rows], axis=0),
        lax.axis_size("item"),
        values,
        table,
        own_table,
        weights,
    )
    padded = 256
    item_q_wide = jnp.zeros((model_width, padded), item_q.dtype).at[:, :model_width].set(item_q)
    unit_lane = (jnp.arange(padded, dtype=jnp.int32) == model_width).astype(jnp.float32)
    queries = jnp.dot(flat_first, item_q_wide, preferred_element_type=jnp.float32)
    queries = (queries + unit_lane[None, :]).astype(jnp.bfloat16)
    shard_count = payload.shape[0] * payload.shape[1]
    payload = payload.reshape(shard_count, dense.shape[0] + COUNT_ROWS, lanes)
    counts = payload[:, dense.shape[0], 0].astype(jnp.int32)
    bias = jnp.where(slot_ids[None, :] < counts[:, None], 0.0, -1e30).reshape(1, -1)
    gathered = payload[:, : dense.shape[0]].reshape(shard_count * EVAL_MAX, model_width)
    keys_t = jnp.einsum(
        "cn,sc->ns", item_kv[:, :model_width], gathered, preferred_element_type=jnp.float32
    ).astype(jnp.bfloat16)
    keys_t = jnp.concatenate(
        [keys_t, bias.astype(jnp.bfloat16), jnp.zeros((padded - model_width - 1, keys_t.shape[1]), jnp.bfloat16)],
        axis=0,
    )
    vals = jnp.dot(
        gathered, item_kv[:, model_width:], preferred_element_type=jnp.float32
    ).astype(jnp.bfloat16)
    vals = jnp.concatenate(
        [vals, jnp.ones((vals.shape[0], 1), jnp.bfloat16), jnp.zeros((vals.shape[0], padded - model_width - 1), jnp.bfloat16)],
        axis=1,
    )
    mixture = row_attention(queries, keys_t, vals)[:, :model_width]
    residual = flat_first.astype(jnp.float32) + jnp.dot(
        mixture, item_out, preferred_element_type=jnp.float32
    )
    second = layer_norm(residual, item_gain).astype(jnp.bfloat16)
    hidden = jax.nn.gelu(
        jnp.dot(second, mlp_in, preferred_element_type=jnp.float32), approximate=True
    ).astype(jnp.bfloat16)
    residual = second.astype(jnp.float32) + jnp.dot(
        hidden, mlp_out, preferred_element_type=jnp.float32
    )
    return (
        layer_norm(residual, mlp_gain)
        .astype(jnp.bfloat16)
        .reshape(row_count, local_groups, model_width)
    )


def solution(mesh):
    in_specs = (
        P("item", None),
        P(),
        P("item"),
        P(),
        P(),
        P(),
        P(),
        P(),
        P(),
        P(),
        P(),
        P(),
        P(),
        P(),
    )
    out_specs = P("item", "grp", None)
    return jax.shard_map(
        per_device, mesh=mesh, in_specs=in_specs, out_specs=out_specs, check_vma=False
    )
```
